256 devices in a mesh: lat: 8 (over x, core), lon: 32 (over z, y).
Axes of the slice: x: 4, y: 4, z: 8, core: 2. Of those that a mesh axis runs over, the one named last changes fastest.
Arguments:
- latent: bfloat16 [64, 8192, 128], P('lat', 'lon'), may hold values from -6 to 6
- head: bfloat16 [128, 32], replicated, may hold values from -0.5 to 0.5
- bias: float32 [32], replicated, may hold values from -3 to 3
- targets: bfloat16 [32, 64, 4096], P(None, 'lat', 'lon'), may hold values from -6 to 6
- margin_cell: int32 [8, 32, 6144], P('lat', 'lon'), may hold values from 0 to 2047
- margin_pixel: int32 [8, 32, 6144], P('lat', 'lon'), may hold values from 0 to 2047, as said below
- margin_weight: float32 [8, 32, 6144], P('lat', 'lon'), may hold values from 0.05 to 1
- live_count: int32 [8, 32], P('lat', 'lon'), may hold values from 2457 to 6144, as said below
Outputs:
- latent_grad: bfloat16 [64, 8192, 128], P('lat', 'lon')
- head_grad: float32 [128, 32], replicated
- bias_grad: float32 [32], replicated
The draws below stay inside these ranges and needn't reach their ends.
Inputs may be any that keep to these rules, and one draw needn't show every extreme that they name: `margin_pixel`: A tile pixel in the device's own band: tile row times (256) plus q, where q - 64 is the column relative to the device's own sector, so q < 64 and q >= 192 are the neighbouring sectors' columns. Both 0 and the largest value occur in every device's list; columns near the frame's edges are covered thinly or not at all. `live_count`: rows at or beyond a device's count are padding and are ignored; in every draw some device has all 6144 rows live.
All inputs are finite; a program needn't handle non-finite values.
Results may differ from the reference program's by a relative error of at most 0.0052.
Values may be sent and summed in bfloat16 or wider, within the bound.
A program may use at most 64 MiB of HBM per device.

```python
import math
import jax
import jax.numpy as jnp
from jax import lax

LATENT = 128
VARS = 32
CR = 8
CC = 256
TX = 128
TY = 8
REACH = 64
ROWS_DEV = 6144
CYCLES = 64
CYCLE_CELLS = 8192
TILE_ROWS = 64
TILE_COLS = 4096
TOTAL_CELLS = 524288
N_LAT = 8
N_LON = 32


def margin_lists(key):
    base_key = jax.random.fold_in(key, 7)
    key_perm, key_extra, key_row, key_col = jax.random.split(base_key, 4)
    device_count = N_LAT * N_LON
    cell_total = CR * CC
    perms = jax.vmap(lambda sub_key: jax.random.permutation(sub_key, cell_total))(jax.random.split(key_perm, device_count)).astype(jnp.int32)
    extra = jax.random.randint(key_extra, (device_count, ROWS_DEV - cell_total), 0, cell_total, dtype=jnp.int32)
    cell_ids = jnp.concatenate([perms, extra], axis=1)
    cycle = cell_ids // CC
    column = cell_ids % CC
    draw_shape = (device_count, ROWS_DEV)
    row_shift = jax.random.randint(key_row, draw_shape, 0, 2, dtype=jnp.int32)
    tile_row = jnp.minimum(cycle * TY // CR + row_shift, TY - 1)
    col_shift = jax.random.randint(key_col, draw_shape, -REACH, REACH + 1, dtype=jnp.int32)
    tile_col = column * TX // CC + col_shift + REACH
    pixel_ids = tile_row * (TX + 2 * REACH) + tile_col
    cell_ids = cell_ids.at[:, 0].set(cell_total - 1)
    pixel_ids = pixel_ids.at[:, 0].set(TY * (TX + 2 * REACH) - 1)
    pixel_ids = pixel_ids.at[:, 1].set(0)
    return (cell_ids.reshape(N_LAT, N_LON, ROWS_DEV), pixel_ids.reshape(N_LAT, N_LON, ROWS_DEV))


def draw_margin_cell(key, part):
    return margin_lists(key)[0]


def draw_margin_pixel(key, part):
    return margin_lists(key)[1]


def draw_live_count(key, part):
    key_count, key_pick = jax.random.split(jax.random.fold_in(key, 13))
    counts = jax.random.randint(key_count, (N_LAT * N_LON,), 2 * ROWS_DEV // 5, ROWS_DEV + 1, dtype=jnp.int32)
    chosen = jax.random.randint(key_pick, (), 0, N_LAT * N_LON, dtype=jnp.int32)
    counts = counts.at[chosen].set(ROWS_DEV)
    return counts.reshape(N_LAT, N_LON)


def steps_of(own_key, extent, pieces, least, high):
    def one(dim, shards_of):
        heights = jax.random.uniform(jax.random.fold_in(jax.random.fold_in(own_key, 6), dim), (shards_of,), jnp.float32, least / len(pieces), high / len(pieces))
        return jnp.repeat(jnp.exp(heights), extent[dim] // shards_of).reshape((-1,) + (1,) * (len(extent) - dim - 1))

    loudness = one(*pieces[0])
    for cut in pieces[1:]:
        loudness = loudness * one(*cut)
    return loudness


def centred(own_key, shape, width, most, shards=(), kind=jnp.bfloat16):
    result = jax.random.normal(own_key, shape, jnp.float32) * width
    if len(shards) > 0:
        result = steps_of(own_key, shape, shards, -0.22, 0.18) * result
    return jnp.clip(result, min=-most, max=most).astype(kind)


def setup_inputs(seed: int = 0) -> dict:
    seeds = jax.random.split(jax.random.key(seed), 9)
    return {
        "latent": centred(seeds[0], (CYCLES, CYCLE_CELLS, LATENT), 1.0, 6.0, ((0, 8), (1, 32))),
        "head": centred(seeds[1], (LATENT, VARS), LATENT ** -0.5, 0.5),
        "bias": centred(seeds[2], (VARS,), 0.5, 3.0, (), jnp.float32),
        "targets": centred(seeds[3], (VARS, TILE_ROWS, TILE_COLS), 1.0, 6.0, ((1, 8), (2, 32))),
        "margin_cell": draw_margin_cell(jax.random.fold_in(seeds[8], 71), 0),
        "margin_pixel": draw_margin_pixel(jax.random.fold_in(seeds[8], 71), 0),
        "margin_weight": jnp.clip(jnp.exp(math.log(1.0) - 2.9957323 * jax.random.uniform(seeds[6], (N_LAT, N_LON, ROWS_DEV), jnp.float32) ** steps_of(seeds[6], (N_LAT, N_LON, ROWS_DEV), ((0, 8), (1, 32)), -0.2, 0.2)), 0.05, 1.0),
        "live_count": draw_live_count(jax.random.fold_in(seeds[8], 71), 0),
    }


def reference(latent, head, bias, targets, margin_cell, margin_pixel, margin_weight, live_count):
    frame_width = TX + 2 * REACH
    row_index = jnp.arange(ROWS_DEV, dtype=jnp.int32)
    sector = jnp.arange(N_LON, dtype=jnp.int32)[:, None]
    grad_bands = []
    head_total = jnp.zeros((LATENT, VARS), jnp.float32)
    bias_total = jnp.zeros((VARS,), jnp.float32)
    for band_index in range(N_LAT):
        band_latent = latent[band_index * CR:(band_index + 1) * CR].reshape(CR * CYCLE_CELLS, LATENT)
        predicted = (jnp.dot(band_latent, head, preferred_element_type=jnp.float32) + bias).astype(jnp.bfloat16)
        local_cell = margin_cell[band_index]
        local_pixel = margin_pixel[band_index]
        cell_index = local_cell // CC * CYCLE_CELLS + sector * CC + local_cell % CC
        pixel_row = local_pixel // frame_width
        pixel_col = local_pixel % frame_width
        pixel_index = pixel_row * TILE_COLS + (sector * TX + pixel_col - REACH) % TILE_COLS
        live_weight = jnp.where(row_index[None, :] < live_count[band_index][:, None], margin_weight[band_index], jnp.float32(0.0))
        cell_flat = cell_index.reshape(-1).astype(jnp.int32)
        pixel_flat = pixel_index.reshape(-1).astype(jnp.int32)
        weight_flat = live_weight.reshape(-1)
        contribution = predicted[cell_flat].astype(jnp.float32) * weight_flat[:, None]
        tiles = jax.ops.segment_sum(contribution, pixel_flat, num_segments=TY * TILE_COLS)
        band_target = targets[:, band_index * TY:(band_index + 1) * TY, :].reshape(VARS, TY * TILE_COLS).T.astype(jnp.float32)
        misfit = tiles - band_target
        backward = misfit[pixel_flat] * weight_flat[:, None]
        cell_misfit = jax.ops.segment_sum(backward, cell_flat, num_segments=CR * CYCLE_CELLS).astype(jnp.bfloat16)
        band_grad = jnp.dot(cell_misfit, head.T, preferred_element_type=jnp.float32).astype(jnp.bfloat16)
        grad_bands.append(band_grad.reshape(CR, CYCLE_CELLS, LATENT))
        head_total = head_total + lax.dot_general(band_latent, cell_misfit, (((0,), (0,)), ((), ())), preferred_element_type=jnp.float32)
        bias_total = bias_total + lax.optimization_barrier(jnp.sum(cell_misfit.astype(jnp.float32), axis=0))
    grad_scale = 1.0 / math.sqrt(TOTAL_CELLS)
    return (jnp.concatenate(grad_bands, axis=0), head_total * grad_scale, bias_total * grad_scale)
```

```python
import functools
import math

import jax
import jax.numpy as jnp
from jax import lax
from jax.experimental import pallas as pl
from jax.experimental.pallas import tpu as pltpu
from jax.sharding import PartitionSpec as P

BF = jnp.bfloat16
F32 = jnp.float32
NT = (((1,), (1,)), ((), ()))
NN = (((1,), (0,)), ((), ()))
GROUPS = (8, 4, 8)


def mm(a, b, dims):
    return lax.dot_general(a, b, dims, preferred_element_type=F32)


def device_of(phase, coord, lat, lon):
    z, y = lon // 4, lon % 4
    if phase == 0:
        return (coord, lon)
    if phase == 1:
        return (lat, z * 4 + coord)
    return (lat, coord * 4 + y)


def kernel(
    scale,
    block,
    live_ref,
    latent_ref,
    head_ref,
    bias_ref,
    targets_ref,
    cell_ref,
    pixel_ref,
    weight_ref,
    grad_ref,
    head_out,
    bias_out,
    onehot_cell,
    onehot_pixel,
    west,
    east,
    from_west,
    from_east,
    cells,
    left,
    right,
    bufs0,
    bufs1,
    bufs2,
    halo_send,
    halo_recv,
    sum_send,
    sum_recv,
):
    lat = lax.axis_index("lat")
    lon = lax.axis_index("lon")
    z, y = lon // 4, lon % 4
    lon_west = lax.rem(lon + 31, 32)
    lon_east = lax.rem(lon + 1, 32)
    mine = (lat, y, z)

    barrier = pltpu.get_barrier_semaphore()
    partners = [(lat, lon_west), (lat, lon_east)]
    for phase, size in enumerate(GROUPS):
        for step in range(1, size):
            partners.append(device_of(phase, lax.rem(mine[phase] + step, size), lat, lon))
    for partner in partners:
        pl.semaphore_signal(barrier, inc=1, device_id=partner, device_id_type=pl.DeviceIdType.MESH)

    rows = cell_ref.shape[1]
    live = live_ref[0, 0]
    sub8 = lax.broadcasted_iota(jnp.int32, (8, block), 0)
    hi_iota = lax.broadcasted_iota(jnp.int32, (256, block), 0)

    repeat = (
        lax.broadcasted_iota(jnp.int32, (256, 32), 0) // 8
        == lax.broadcasted_iota(jnp.int32, (256, 32), 1)
    )
    repeat_bf = jnp.where(repeat, 1.0, 0.0).astype(BF)
    head_rep = mm(repeat_bf, head_ref[...], NN)
    bias_rep = jnp.sum(jnp.where(repeat, bias_ref[...], 0.0), axis=1, keepdims=True)
    low_of = lax.broadcasted_iota(jnp.int32, (256, 128), 0) % 8
    head_low = [jnp.where(low_of == low, head_rep, 0.0).astype(BF) for low in range(8)]

    predicted = jnp.zeros((256, 256), F32)
    for low in range(0, 8, 2):
        predicted += mm(
            jnp.concatenate([head_low[low], head_low[low + 1]], axis=1),
            jnp.concatenate([latent_ref[low], latent_ref[low + 1]], axis=1),
            NT,
        )
    predicted = (predicted + bias_rep).astype(BF)

    same_var = (
        lax.broadcasted_iota(jnp.int32, (256, 256), 0) // 8
        == lax.broadcasted_iota(jnp.int32, (256, 256), 1) // 8
    )
    collapse = jnp.where(same_var, 1.0, 0.0).astype(BF)

    def move(picked, low_from, low_to, weight):
        mask_from = jnp.where(sub8 == low_from, 1.0, 0.0)[None]
        chosen = (picked.reshape(32, 8, block) * mask_from).reshape(256, block).astype(BF)
        spread = mm(collapse, chosen, NN)
        scaled = jnp.where(sub8 == low_to, weight, 0.0)[None]
        return (spread.reshape(32, 8, block) * scaled).reshape(256, block).astype(BF)

    def row_block(step):
        span = pl.ds(pl.multiple_of(step * block, block), block)
        cell = cell_ref[:, span]
        pixel = pixel_ref[:, span]
        index = lax.broadcasted_iota(jnp.int32, (1, block), 1) + step * block
        weight = jnp.where(index < live, weight_ref[:, span], 0.0)
        return span, cell, pixel, weight

    west[...] = jnp.zeros_like(west)
    east[...] = jnp.zeros_like(east)
    rolled = pltpu.roll(targets_ref[...].astype(F32), 64, 1)
    lane = lax.broadcasted_iota(jnp.int32, (256, 128), 1)
    cells[:, :128] = jnp.where(lane >= 64, -rolled, 0.0)
    cells[:, 128:] = jnp.where(lane < 64, -rolled, 0.0)

    def forward(step, carry):
        span, cell, pixel, weight = row_block(step)
        hot_cell = jnp.where(hi_iota == (cell & 255), 1.0, 0.0).astype(BF)
        hot_pixel = jnp.where(hi_iota == (pixel & 255), 1.0, 0.0).astype(BF)
        onehot_cell[:, span] = hot_cell
        onehot_pixel[:, span] = hot_pixel
        picked = mm(predicted, hot_cell, NN)
        moved = move(picked, cell >> 8, pixel >> 8, weight)
        cells[...] += mm(moved, hot_pixel, NT)
        return carry

    lax.fori_loop(0, rows // block, forward, 0)
    west[...] = cells[:, :128].astype(BF)
    east[...] = cells[:, 128:].astype(BF)

    pl.semaphore_wait(barrier, len(partners))
    to_west = pltpu.make_async_remote_copy(
        src_ref=west,
        dst_ref=from_east,
        send_sem=halo_send.at[0],
        recv_sem=halo_recv.at[0],
        device_id=(lat, lon_west),
        device_id_type=pl.DeviceIdType.MESH,
    )
    to_east = pltpu.make_async_remote_copy(
        src_ref=east,
        dst_ref=from_west,
        send_sem=halo_send.at[1],
        recv_sem=halo_recv.at[1],
        device_id=(lat, lon_east),
        device_id_type=pl.DeviceIdType.MESH,
    )
    to_west.start()
    to_east.start()
    to_west.wait()
    to_east.wait()
    misfit = jnp.concatenate(
        [
            (cells[:, :128] + from_west[...].astype(F32)).astype(BF),
            (cells[:, 128:] + from_east[...].astype(F32)).astype(BF),
        ],
        axis=1,
    )
    cells[...] = jnp.zeros_like(cells)

    def backward(step, carry):
        span, cell, pixel, weight = row_block(step)
        picked = mm(misfit, onehot_pixel[:, span], NN)
        moved = move(picked, pixel >> 8, cell >> 8, weight)
        cells[...] += mm(moved, onehot_cell[:, span], NT)
        return carry

    lax.fori_loop(0, rows // block, backward, 0)

    left[...] = cells[:, :128]
    right[...] = cells[:, 128:]
    head_part = jnp.zeros((32, 128), F32)
    bias_part = jnp.zeros((8, 32), F32)
    ones = jnp.ones((8, 256), BF)
    for low in range(8):
        every = pl.ds(low, 32, stride=8)
        of_low = jnp.concatenate([left[every, :], right[every, :]], axis=1).astype(BF)
        head_part += mm(of_low, latent_ref[low], NN)
        bias_part += mm(ones, of_low, NT)

    all_bufs = (bufs0, bufs1, bufs2)
    total_head, total_bias = head_part, bias_part
    first = 0
    for phase, size in enumerate(GROUPS):
        bufs, me = all_bufs[phase], mine[phase]
        bufs[me, :32, :] = total_head.astype(BF)
        bufs[me, 32:, :] = jnp.zeros((16, 128), BF)
        bufs[me, 32:40, :32] = total_bias.astype(BF)
        copies = []
        for step in range(1, size):
            copy = pltpu.make_async_remote_copy(
                src_ref=bufs.at[me],
                dst_ref=bufs.at[me],
                send_sem=sum_send.at[first],
                recv_sem=sum_recv.at[first],
                device_id=device_of(phase, lax.rem(me + step, size), lat, lon),
                device_id_type=pl.DeviceIdType.MESH,
            )
            copy.start()
            copies.append(copy)
            first += 1
        if phase == 0:
            turned = cells[...].T.astype(BF)
            for low in range(8):
                grad_ref[low] = mm(turned, head_low[low], NN).astype(BF)
        for copy in copies:
            copy.wait()
        total_head = bufs[0, :32, :].astype(F32)
        total_bias = bufs[0, 32:40, :32].astype(F32)
        for other in range(1, size):
            total_head += bufs[other, :32, :].astype(F32)
            total_bias += bufs[other, 32:40, :32].astype(F32)

    head_out[...] = total_head * scale
    bias_out[...] = total_bias[:1, :] * scale


def per_device(latent, head, bias, targets, margin_cell, margin_pixel, margin_weight, live_count):
    rows = margin_cell.shape[-1]
    scale = 1.0 / math.sqrt(524288)
    block = 512
    vmem = pl.BlockSpec(memory_space=pltpu.VMEM)
    smem = pl.BlockSpec(memory_space=pltpu.SMEM)
    copies = sum(size - 1 for size in GROUPS)
    grad, head_grad, bias_grad = pl.pallas_call(
        functools.partial(kernel, scale, block),
        out_shape=(
            jax.ShapeDtypeStruct(latent.shape, BF),
            jax.ShapeDtypeStruct((32, 128), F32),
            jax.ShapeDtypeStruct((1, 32), F32),
        ),
        in_specs=[smem] + [vmem] * 7,
        out_specs=(vmem, vmem, vmem),
        scratch_shapes=[
            pltpu.VMEM((256, rows), BF),
            pltpu.VMEM((256, rows), BF),
            pltpu.VMEM((256, 128), BF),
            pltpu.VMEM((256, 128), BF),
            pltpu.VMEM((256, 128), BF),
            pltpu.VMEM((256, 128), BF),
            pltpu.VMEM((256, 256), F32),
            pltpu.VMEM((256, 128), F32),
            pltpu.VMEM((256, 128), F32),
            pltpu.VMEM((8, 48, 128), BF),
            pltpu.VMEM((4, 48, 128), BF),
            pltpu.VMEM((8, 48, 128), BF),
            pltpu.SemaphoreType.DMA((2,)),
            pltpu.SemaphoreType.DMA((2,)),
            pltpu.SemaphoreType.DMA((copies,)),
            pltpu.SemaphoreType.DMA((copies,)),
        ],
        compiler_params=pltpu.CompilerParams(
            collective_id=0, has_side_effects=True, vmem_limit_bytes=48 * 1024 * 1024
        ),
    )(
        live_count,
        latent,
        head.T,
        bias.reshape(1, 32),
        targets.reshape(256, 128),
        margin_cell.reshape(1, rows),
        margin_pixel.reshape(1, rows),
        margin_weight.reshape(1, rows),
    )
    return grad, head_grad.T, bias_grad.reshape(32)


def solution(mesh):
    lat, lon = "lat", "lon"
    in_specs = (
        P(lat, lon, None),
        P(),
        P(),
        P(None, lat, lon),
        P(lat, lon, None),
        P(lat, lon, None),
        P(lat, lon, None),
        P(lat, lon),
    )
    out_specs = (P(lat, lon, None), P(), P())
    return jax.shard_map(
        per_device, mesh=mesh, in_specs=in_specs, out_specs=out_specs, check_vma=False
    )
```

```python
import functools
import math

import jax
import jax.numpy as jnp
from jax import lax
from jax.experimental import pallas as pl
from jax.experimental.pallas import tpu as pltpu
from jax.sharding import PartitionSpec as P

BF = jnp.bfloat16
F32 = jnp.float32
NT = (((1,), (1,)), ((), ()))
NN = (((1,), (0,)), ((), ()))
GROUPS = (8, 4, 8)


def mm(a, b, dims):
    return lax.dot_general(a, b, dims, preferred_element_type=F32)


def device_of(phase, coord, lat, lon):
    z, y = lon // 4, lon % 4
    if phase == 0:
        return (coord, lon)
    if phase == 1:
        return (lat, z * 4 + coord)
    return (lat, coord * 4 + y)


def kernel(
    scale,
    block,
    live_in,
    latent_in,
    head_in,
    bias_in,
    targets_in,
    cell_in,
    pixel_in,
    weight_in,
    grad_ref,
    head_out,
    bias_out,
    onehot_cell,
    onehot_pixel,
    west,
    east,
    from_west,
    from_east,
    cells,
    left,
    right,
    bufs0,
    bufs1,
    bufs2,
    halo_send,
    halo_recv,
    sum_send,
    sum_recv,
    latent_ref,
    head_ref,
    bias_ref,
    targets_ref,
    cell_ref,
    pixel_ref,
    weight_ref,
    load_sem,
):
    pairs = (
        (cell_in, cell_ref),
        (pixel_in, pixel_ref),
        (weight_in, weight_ref),
        (head_in, head_ref),
        (bias_in, bias_ref),
        (latent_in, latent_ref),
        (targets_in, targets_ref),
    )
    loads = []
    for slot, (source, target) in enumerate(pairs):
        load = pltpu.make_async_copy(source, target, load_sem.at[slot])
        load.start()
        loads.append(load)
    lat = lax.axis_index("lat")
    lon = lax.axis_index("lon")
    z, y = lon // 4, lon % 4
    lon_west = lax.rem(lon + 31, 32)
    lon_east = lax.rem(lon + 1, 32)
    mine = (lat, y, z)

    barrier = pltpu.get_barrier_semaphore()
    partners = [(lat, lon_west), (lat, lon_east)]
    for phase, size in enumerate(GROUPS):
        for step in range(1, size):
            partners.append(device_of(phase, lax.rem(mine[phase] + step, size), lat, lon))
    for partner in partners:
        pl.semaphore_signal(barrier, inc=1, device_id=partner, device_id_type=pl.DeviceIdType.MESH)

    rows = cell_ref.shape[1]
    sub8 = lax.broadcasted_iota(jnp.int32, (8, block), 0)
    hi_iota = lax.broadcasted_iota(jnp.int32, (256, block), 0).astype(F32).astype(BF)

    for load in loads:
        load.wait()
    live = live_in[0, 0]

    repeat = (
        lax.broadcasted_iota(jnp.int32, (256, 32), 0) // 8
        == lax.broadcasted_iota(jnp.int32, (256, 32), 1)
    )
    repeat_bf = jnp.where(repeat, 1.0, 0.0).astype(BF)
    head_rep = mm(repeat_bf, head_ref[...], NN)
    bias_rep = jnp.sum(jnp.where(repeat, bias_ref[...], 0.0), axis=1, keepdims=True)
    low_of = lax.broadcasted_iota(jnp.int32, (256, 128), 0) % 8
    head_low = [jnp.where(low_of == low, head_rep, 0.0).astype(BF) for low in range(8)]

    predicted = jnp.zeros((256, 256), F32)
    for low in range(0, 8, 2):
        predicted += mm(
            jnp.concatenate([head_low[low], head_low[low + 1]], axis=1),
            jnp.concatenate([latent_ref[low], latent_ref[low + 1]], axis=1),
            NT,
        )
    predicted = (predicted + bias_rep).astype(BF)

    same_var = (
        lax.broadcasted_iota(jnp.int32, (256, 256), 0) // 8
        == lax.broadcasted_iota(jnp.int32, (256, 256), 1) // 8
    )
    collapse = jnp.where(same_var, 1.0, 0.0).astype(BF)

    def move(picked, low_from, low_to, weight):
        source = jnp.broadcast_to(low_from, (8, block))
        scaled = jnp.where(sub8 == low_to, weight, 0.0)
        return jnp.concatenate(
            [
                jnp.take_along_axis(picked[8 * v : 8 * v + 8], source, axis=0) * scaled
                for v in range(32)
            ],
            axis=0,
        ).astype(BF)

    def hot(index):
        high = jnp.broadcast_to((index & 255).astype(F32).astype(BF), (256, block))
        return jnp.where(hi_iota == high, jnp.ones((), BF), jnp.zeros((), BF))

    def row_block(step):
        span = pl.ds(step * block, block)
        cell = cell_ref[:, span]
        pixel = pixel_ref[:, span]
        index = lax.broadcasted_iota(jnp.int32, (1, block), 1) + step * block
        weight = jnp.where(index < live, weight_ref[:, span], 0.0)
        return span, cell, pixel, weight

    west[...] = jnp.zeros_like(west)
    east[...] = jnp.zeros_like(east)
    rolled = pltpu.roll(targets_ref[...].astype(F32), 64, 1)
    lane = lax.broadcasted_iota(jnp.int32, (256, 128), 1)
    cells[:, :128] = jnp.where(lane >= 64, -rolled, 0.0)
    cells[:, 128:] = jnp.where(lane < 64, -rolled, 0.0)

    def forward(step, carry):
        span, cell, pixel, weight = row_block(step)
        hot_cell = hot(cell)
        hot_pixel = hot(pixel)
        onehot_cell[:, span] = hot_cell
        onehot_pixel[:, span] = hot_pixel
        picked = mm(predicted, hot_cell, NN)
        moved = move(picked, cell >> 8, pixel >> 8, weight)
        cells[...] += mm(moved, hot_pixel, NT)
        return carry

    [forward(k, 0) for k in range(rows // block)]
    west[...] = cells[:, :128].astype(BF)
    east[...] = cells[:, 128:].astype(BF)

    pl.semaphore_wait(barrier, len(partners))
    to_west = pltpu.make_async_remote_copy(
        src_ref=west,
        dst_ref=from_east,
        send_sem=halo_send.at[0],
        recv_sem=halo_recv.at[0],
        device_id=(lat, lon_west),
        device_id_type=pl.DeviceIdType.MESH,
    )
    to_east = pltpu.make_async_remote_copy(
        src_ref=east,
        dst_ref=from_west,
        send_sem=halo_send.at[1],
        recv_sem=halo_recv.at[1],
        device_id=(lat, lon_east),
        device_id_type=pl.DeviceIdType.MESH,
    )
    to_west.start()
    to_east.start()
    to_west.wait()
    to_east.wait()
    misfit = jnp.concatenate(
        [
            (cells[:, :128] + from_west[...].astype(F32)).astype(BF),
            (cells[:, 128:] + from_east[...].astype(F32)).astype(BF),
        ],
        axis=1,
    )
    cells[...] = jnp.zeros_like(cells)

    def backward(step, carry):
        span, cell, pixel, weight = row_block(step)
        picked = mm(misfit, onehot_pixel[:, span], NN)
        moved = move(picked, pixel >> 8, cell >> 8, weight)
        cells[...] += mm(moved, onehot_cell[:, span], NT)
        return carry

    [backward(k, 0) for k in range(rows // block)]

    left[...] = cells[:, :128]
    right[...] = cells[:, 128:]
    head_part = jnp.zeros((32, 128), F32)
    bias_part = jnp.zeros((8, 32), F32)
    ones = jnp.ones((8, 256), BF)
    for low in range(8):
        every = pl.ds(low, 32, stride=8)
        of_low = jnp.concatenate([left[every, :], right[every, :]], axis=1).astype(BF)
        head_part += mm(of_low, latent_ref[low], NN)
        bias_part += mm(ones, of_low, NT)

    all_bufs = (bufs0, bufs1, bufs2)
    total_head, total_bias = head_part, bias_part
    first = 0
    for phase, size in enumerate(GROUPS):
        bufs, me = all_bufs[phase], mine[phase]
        bufs[me, :32, :] = total_head.astype(BF)
        bufs[me, 32:, :] = jnp.zeros((16, 128), BF)
        bufs[me, 32:40, :32] = total_bias.astype(BF)
        copies = []
        for step in range(1, size):
            copy = pltpu.make_async_remote_copy(
                src_ref=bufs.at[me],
                dst_ref=bufs.at[me],
                send_sem=sum_send.at[first],
                recv_sem=sum_recv.at[first],
                device_id=device_of(phase, lax.rem(me + step, size), lat, lon),
                device_id_type=pl.DeviceIdType.MESH,
            )
            copy.start()
            copies.append(copy)
            first += 1
        if phase == 0:
            turned = cells[...].T.astype(BF)
            for low in range(8):
                grad_ref[low] = mm(turned, head_low[low], NN).astype(BF)
        for copy in copies:
            copy.wait()
        total_head = bufs[0, :32, :].astype(F32)
        total_bias = bufs[0, 32:40, :32].astype(F32)
        for other in range(1, size):
            total_head += bufs[other, :32, :].astype(F32)
            total_bias += bufs[other, 32:40, :32].astype(F32)

    head_out[...] = total_head * scale
    bias_out[...] = total_bias[:1, :] * scale


def write_kernel(grad_in, head_in, bias_in, grad_out, head_out, bias_out, sem):
    copies = []
    for slot, (source, target) in enumerate(
        ((grad_in, grad_out), (head_in, head_out), (bias_in, bias_out))
    ):
        copy = pltpu.make_async_copy(source, target, sem.at[slot])
        copy.start()
        copies.append(copy)
    for copy in copies:
        copy.wait()


def write_out(*arrays):
    return pl.pallas_call(
        write_kernel,
        out_shape=tuple(jax.ShapeDtypeStruct(a.shape, a.dtype) for a in arrays),
        in_specs=[pl.BlockSpec(memory_space=pltpu.VMEM)] * 3,
        out_specs=(pl.BlockSpec(memory_space=pl.ANY),) * 3,
        scratch_shapes=[pltpu.SemaphoreType.DMA((3,))],
        compiler_params=pltpu.CompilerParams(vmem_limit_bytes=1024 * 1024),
    )(*arrays)


def per_device(latent, head, bias, targets, margin_cell, margin_pixel, margin_weight, live_count):
    rows = margin_cell.shape[-1]
    scale = 1.0 / math.sqrt(524288)
    block = 512
    vmem = pl.BlockSpec(memory_space=pltpu.VMEM)
    copies = sum(size - 1 for size in GROUPS)
    grad, head_grad, bias_grad = pl.pallas_call(
        functools.partial(kernel, scale, block),
        out_shape=(
            jax.ShapeDtypeStruct(latent.shape, BF),
            jax.ShapeDtypeStruct((32, 128), F32),
            jax.ShapeDtypeStruct((1, 32), F32),
        ),
        in_specs=[pl.BlockSpec(memory_space=pltpu.SMEM)] + [pl.BlockSpec(memory_space=pltpu.HBM)] * 7,
        out_specs=(vmem, vmem, vmem),
        scratch_shapes=[
            pltpu.VMEM((256, rows), BF),
            pltpu.VMEM((256, rows), BF),
            pltpu.VMEM((256, 128), BF),
            pltpu.VMEM((256, 128), BF),
            pltpu.VMEM((256, 128), BF),
            pltpu.VMEM((256, 128), BF),
            pltpu.VMEM((256, 256), F32),
            pltpu.VMEM((256, 128), F32),
            pltpu.VMEM((256, 128), F32),
            pltpu.VMEM((8, 48, 128), BF),
            pltpu.VMEM((4, 48, 128), BF),
            pltpu.VMEM((8, 48, 128), BF),
            pltpu.SemaphoreType.DMA((2,)),
            pltpu.SemaphoreType.DMA((2,)),
            pltpu.SemaphoreType.DMA((copies,)),
            pltpu.SemaphoreType.DMA((copies,)),
            pltpu.VMEM(latent.shape, BF),
            pltpu.VMEM((32, 128), BF),
            pltpu.VMEM((1, 32), F32),
            pltpu.VMEM((256, 128), BF),
            pltpu.VMEM((1, rows), jnp.int32),
            pltpu.VMEM((1, rows), jnp.int32),
            pltpu.VMEM((1, rows), F32),
            pltpu.SemaphoreType.DMA((8,)),
        ],
        compiler_params=pltpu.CompilerParams(
            collective_id=0, has_side_effects=True, vmem_limit_bytes=32 * 1024 * 1024
        ),
    )(
        live_count,
        *[
            pltpu.with_memory_space_constraint(operand, pltpu.HBM)
            for operand in (
                latent,
                head.T,
                bias.reshape(1, 32),
                targets.reshape(256, 128),
                margin_cell.reshape(1, rows),
                margin_pixel.reshape(1, rows),
                margin_weight.reshape(1, rows),
            )
        ]
    )
    grad, head_grad, bias_grad = write_out(grad, head_grad, bias_grad)
    return grad, head_grad.T, bias_grad.reshape(32)


def solution(mesh):
    lat, lon = "lat", "lon"
    in_specs = (
        P(lat, lon, None),
        P(),
        P(),
        P(None, lat, lon),
        P(lat, lon, None),
        P(lat, lon, None),
        P(lat, lon, None),
        P(lat, lon),
    )
    out_specs = (P(lat, lon, None), P(), P())
    return jax.shard_map(
        per_device, mesh=mesh, in_specs=in_specs, out_specs=out_specs, check_vma=False
    )
```

```python
import functools
import math

import jax
import jax.numpy as jnp
from jax import lax
from jax.experimental import pallas as pl
from jax.experimental.pallas import tpu as pltpu
from jax.sharding import PartitionSpec as P

BF = jnp.bfloat16
F32 = jnp.float32
NT = (((1,), (1,)), ((), ()))
NN = (((1,), (0,)), ((), ()))
GROUPS = (8, 4, 8)


def mm(a, b, dims):
    return lax.dot_general(a, b, dims, preferred_element_type=F32)


def device_of(phase, coord, lat, lon):
    z, y = lon // 4, lon % 4
    if phase == 0:
        return (coord, lon)
    if phase == 1:
        return (lat, z * 4 + coord)
    return (lat, coord * 4 + y)


def kernel(
    scale,
    block,
    live_in,
    latent_in,
    head_in,
    bias_in,
    targets_in,
    cell_in,
    pixel_in,
    weight_in,
    grad_ref,
    head_out,
    bias_out,
    onehot_cell,
    onehot_pixel,
    west,
    east,
    from_west,
    from_east,
    cells,
    left,
    right,
    bufs0,
    bufs1,
    bufs2,
    halo_send,
    halo_recv,
    sum_send,
    sum_recv,
    latent_ref,
    head_ref,
    bias_ref,
    targets_ref,
    cell_ref,
    pixel_ref,
    weight_ref,
    load_sem,
):
    pairs = (
        (cell_in, cell_ref),
        (pixel_in, pixel_ref),
        (weight_in, weight_ref),
        (head_in, head_ref),
        (bias_in, bias_ref),
        (latent_in, latent_ref),
        (targets_in, targets_ref),
    )
    loads = []
    for slot, (source, target) in enumerate(pairs):
        load = pltpu.make_async_copy(source, target, load_sem.at[slot])
        load.start()
        loads.append(load)
    lat = lax.axis_index("lat")
    lon = lax.axis_index("lon")
    z, y = lon // 4, lon % 4
    lon_west = lax.rem(lon + 31, 32)
    lon_east = lax.rem(lon + 1, 32)
    mine = (lat, y, z)

    barrier = pltpu.get_barrier_semaphore()
    partners = [(lat, lon_west), (lat, lon_east)]
    for phase, size in enumerate(GROUPS):
        for step in range(1, size):
            partners.append(device_of(phase, lax.rem(mine[phase] + step, size), lat, lon))
    for partner in partners:
        pl.semaphore_signal(barrier, inc=1, device_id=partner, device_id_type=pl.DeviceIdType.MESH)

    rows = cell_ref.shape[1]
    sub8 = lax.broadcasted_iota(jnp.int32, (8, block), 0)
    hi_iota = lax.broadcasted_iota(jnp.int32, (256, block), 0).astype(F32).astype(BF)

    for load in loads:
        load.wait()
    live = live_in[0, 0]

    repeat = (
        lax.broadcasted_iota(jnp.int32, (256, 32), 0) // 8
        == lax.broadcasted_iota(jnp.int32, (256, 32), 1)
    )
    repeat_bf = jnp.where(repeat, 1.0, 0.0).astype(BF)
    head_rep = mm(repeat_bf, head_ref[...], NN)
    bias_rep = jnp.sum(jnp.where(repeat, bias_ref[...], 0.0), axis=1, keepdims=True)
    low_of = lax.broadcasted_iota(jnp.int32, (256, 128), 0) % 8
    head_low = [jnp.where(low_of == low, head_rep, 0.0).astype(BF) for low in range(8)]

    predicted = jnp.zeros((256, 256), F32)
    for low in range(0, 8, 2):
        predicted += mm(
            jnp.concatenate([head_low[low], head_low[low + 1]], axis=1),
            jnp.concatenate([latent_ref[low], latent_ref[low + 1]], axis=1),
            NT,
        )
    predicted = (predicted + bias_rep).astype(BF)

    same_var = (
        lax.broadcasted_iota(jnp.int32, (256, 256), 0) // 8
        == lax.broadcasted_iota(jnp.int32, (256, 256), 1) // 8
    )
    collapse = jnp.where(same_var, 1.0, 0.0).astype(BF)

    def move(picked, low_from, low_to, weight):
        source = jnp.broadcast_to(low_from, (8, block))
        scaled = jnp.where(sub8 == low_to, weight, 0.0)
        return jnp.concatenate(
            [
                jnp.take_along_axis(picked[8 * v : 8 * v + 8], source, axis=0) * scaled
                for v in range(32)
            ],
            axis=0,
        ).astype(BF)

    def hot(index):
        high = jnp.broadcast_to((index & 255).astype(F32).astype(BF), (256, block))
        return jnp.where(hi_iota == high, jnp.ones((), BF), jnp.zeros((), BF))

    def row_block(step):
        span = pl.ds(step * block, block)
        cell = cell_ref[:, span]
        pixel = pixel_ref[:, span]
        index = lax.broadcasted_iota(jnp.int32, (1, block), 1) + step * block
        weight = jnp.where(index < live, weight_ref[:, span], 0.0)
        return span, cell, pixel, weight

    west[...] = jnp.zeros_like(west)
    east[...] = jnp.zeros_like(east)
    rolled = pltpu.roll(targets_ref[...].astype(F32), 64, 1)
    lane = lax.broadcasted_iota(jnp.int32, (256, 128), 1)
    cells[:, :128] = jnp.where(lane >= 64, -rolled, 0.0)
    cells[:, 128:] = jnp.where(lane < 64, -rolled, 0.0)

    def forward(step, carry):
        span, cell, pixel, weight = row_block(step)
        hot_cell = hot(cell)
        hot_pixel = hot(pixel)
        onehot_cell[:, span] = hot_cell
        onehot_pixel[:, span] = hot_pixel
        picked = mm(predicted, hot_cell, NN)
        moved = move(picked, cell >> 8, pixel >> 8, weight)
        cells[...] += mm(moved, hot_pixel, NT)
        return carry

    [forward(k, 0) for k in range(rows // block)]
    west[...] = cells[:, :128].astype(BF)
    east[...] = cells[:, 128:].astype(BF)

    pl.semaphore_wait(barrier, len(partners))
    to_west = pltpu.make_async_remote_copy(
        src_ref=west,
        dst_ref=from_east,
        send_sem=halo_send.at[0],
        recv_sem=halo_recv.at[0],
        device_id=(lat, lon_west),
        device_id_type=pl.DeviceIdType.MESH,
    )
    to_east = pltpu.make_async_remote_copy(
        src_ref=east,
        dst_ref=from_west,
        send_sem=halo_send.at[1],
        recv_sem=halo_recv.at[1],
        device_id=(lat, lon_east),
        device_id_type=pl.DeviceIdType.MESH,
    )
    to_west.start()
    to_east.start()
    to_west.wait()
    to_east.wait()
    misfit = jnp.concatenate(
        [
            (cells[:, :128] + from_west[...].astype(F32)).astype(BF),
            (cells[:, 128:] + from_east[...].astype(F32)).astype(BF),
        ],
        axis=1,
    )
    cells[...] = jnp.zeros_like(cells)

    def backward(step, carry):
        span, cell, pixel, weight = row_block(step)
        picked = mm(misfit, onehot_pixel[:, span], NN)
        moved = move(picked, pixel >> 8, cell >> 8, weight)
        cells[...] += mm(moved, onehot_cell[:, span], NT)
        return carry

    [backward(k, 0) for k in range(rows // block)]

    left[...] = cells[:, :128]
    right[...] = cells[:, 128:]
    head_part = jnp.zeros((32, 128), F32)
    bias_part = jnp.zeros((8, 32), F32)
    ones = jnp.ones((8, 256), BF)
    for low in range(8):
        every = pl.ds(low, 32, stride=8)
        of_low = jnp.concatenate([left[every, :], right[every, :]], axis=1).astype(BF)
        head_part += mm(of_low, latent_ref[low], NN)
        bias_part += mm(ones, of_low, NT)

    bias8 = jnp.concatenate([bias_part, jnp.zeros((8, 96), F32)], axis=1)
    total = jnp.concatenate([head_part, bias8], axis=0).reshape(5, 8, 128)
    first = 0
    for phase, (bufs, size) in enumerate(zip((bufs0, bufs1, bufs2), GROUPS)):
        me = mine[phase]
        bufs[me] = total.astype(BF)
        copies = []
        for order in range(size - 1):
            other = order + jnp.where(order >= me, 1, 0)
            copy = pltpu.make_async_remote_copy(
                src_ref=bufs.at[me],
                dst_ref=bufs.at[me],
                send_sem=sum_send.at[first + order],
                recv_sem=sum_recv.at[first + me],
                device_id=device_of(phase, other, lat, lon),
                device_id_type=pl.DeviceIdType.MESH,
            )
            copy.start()
            arrival = pltpu.make_async_remote_copy(
                src_ref=bufs.at[other],
                dst_ref=bufs.at[other],
                send_sem=sum_send.at[first + order],
                recv_sem=sum_recv.at[first + other],
                device_id=device_of(phase, other, lat, lon),
                device_id_type=pl.DeviceIdType.MESH,
            )
            copies.append((copy, arrival))
        if phase == 0:
            turned = cells[...].T.astype(BF)
            for low in range(8):
                grad_ref[low] = mm(turned, head_low[low], NN).astype(BF)
        for copy, arrival in copies:
            arrival.wait_recv()
        total = bufs[0].astype(F32)
        for other in range(1, size):
            total += bufs[other].astype(F32)
        for copy, arrival in copies:
            copy.wait_send()
        first += size

    for group in range(4):
        head_out[8 * group : 8 * group + 8] = total[group] * scale
    bias_out[...] = total[4][:1, :32] * scale


def write_kernel(grad_in, head_in, bias_in, grad_out, head_out, bias_out, sem):
    copies = []
    for slot, (source, target) in enumerate(
        ((grad_in, grad_out), (head_in, head_out), (bias_in, bias_out))
    ):
        copy = pltpu.make_async_copy(source, target, sem.at[slot])
        copy.start()
        copies.append(copy)
    for copy in copies:
        copy.wait()


def write_out(*arrays):
    return pl.pallas_call(
        write_kernel,
        out_shape=tuple(jax.ShapeDtypeStruct(a.shape, a.dtype) for a in arrays),
        in_specs=[pl.BlockSpec(memory_space=pltpu.VMEM)] * 3,
        out_specs=(pl.BlockSpec(memory_space=pl.ANY),) * 3,
        scratch_shapes=[pltpu.SemaphoreType.DMA((3,))],
        compiler_params=pltpu.CompilerParams(vmem_limit_bytes=1024 * 1024),
    )(*arrays)


def per_device(latent, head, bias, targets, margin_cell, margin_pixel, margin_weight, live_count):
    rows = margin_cell.shape[-1]
    scale = 1.0 / math.sqrt(524288)
    block = 512
    vmem = pl.BlockSpec(memory_space=pltpu.VMEM)
    copies = sum(GROUPS)
    grad, head_grad, bias_grad = pl.pallas_call(
        functools.partial(kernel, scale, block),
        out_shape=(
            jax.ShapeDtypeStruct(latent.shape, BF),
            jax.ShapeDtypeStruct((32, 128), F32),
            jax.ShapeDtypeStruct((1, 32), F32),
        ),
        in_specs=[pl.BlockSpec(memory_space=pltpu.SMEM)] + [pl.BlockSpec(memory_space=pltpu.HBM)] * 7,
        out_specs=(vmem, vmem, vmem),
        scratch_shapes=[
            pltpu.VMEM((256, rows), BF),
            pltpu.VMEM((256, rows), BF),
            pltpu.VMEM((256, 128), BF),
            pltpu.VMEM((256, 128), BF),
            pltpu.VMEM((256, 128), BF),
            pltpu.VMEM((256, 128), BF),
            pltpu.VMEM((256, 256), F32),
            pltpu.VMEM((256, 128), F32),
            pltpu.VMEM((256, 128), F32),
            pltpu.VMEM((8, 5, 8, 128), BF),
            pltpu.VMEM((4, 5, 8, 128), BF),
            pltpu.VMEM((8, 5, 8, 128), BF),
            pltpu.SemaphoreType.DMA((2,)),
            pltpu.SemaphoreType.DMA((2,)),
            pltpu.SemaphoreType.DMA((copies,)),
            pltpu.SemaphoreType.DMA((copies,)),
            pltpu.VMEM(latent.shape, BF),
            pltpu.VMEM((32, 128), BF),
            pltpu.VMEM((1, 32), F32),
            pltpu.VMEM((256, 128), BF),
            pltpu.VMEM((1, rows), jnp.int32),
            pltpu.VMEM((1, rows), jnp.int32),
            pltpu.VMEM((1, rows), F32),
            pltpu.SemaphoreType.DMA((8,)),
        ],
        compiler_params=pltpu.CompilerParams(
            collective_id=0, has_side_effects=True, vmem_limit_bytes=32 * 1024 * 1024
        ),
    )(
        live_count,
        *[
            pltpu.with_memory_space_constraint(operand, pltpu.HBM)
            for operand in (
                latent,
                head.T,
                bias.reshape(1, 32),
                targets.reshape(256, 128),
                margin_cell.reshape(1, rows),
                margin_pixel.reshape(1, rows),
                margin_weight.reshape(1, rows),
            )
        ]
    )
    grad, head_grad, bias_grad = write_out(grad, head_grad, bias_grad)
    return grad, head_grad.T, bias_grad.reshape(32)


def solution(mesh):
    lat, lon = "lat", "lon"
    in_specs = (
        P(lat, lon, None),
        P(),
        P(),
        P(None, lat, lon),
        P(lat, lon, None),
        P(lat, lon, None),
        P(lat, lon, None),
        P(lat, lon),
    )
    out_specs = (P(lat, lon, None), P(), P())
    return jax.shard_map(
        per_device, mesh=mesh, in_specs=in_specs, out_specs=out_specs, check_vma=False
    )
```
